512 devices in a mesh: seqhi: 16 (over z_lo, core), seqlo: 32 (over y, z_hi, x).
Axes of the slice: x: 4, y: 4, z: 16 (z_hi: 2, z_lo: 8; z = z_hi * 8 + z_lo), core: 2. Of those that a mesh axis runs over, the one named last changes fastest.
Arguments:
- features: float32 [131072, 256], P(('seqhi', 'seqlo')), may hold values from -6 to 6
- norm_gain: float32 [8, 512], replicated, may hold values from 0.1 to 1.9
- bias_hidden: float32 [8, 1024], replicated, may hold values from -4 to 4
- gate_logit: float32 [8, 512], replicated, may hold values from -2 to 2
- w_in: float32 [512, 1024], replicated, may hold values from -0.25 to 0.25
- w_out: float32 [1024, 512], replicated, may hold values from -0.1875 to 0.1875
Outputs:
- switched: float32 [131072, 256], P(('seqhi', 'seqlo'))
The draws below stay inside these ranges and needn't reach their ends.
All inputs are finite; a program needn't handle non-finite values.
Results may differ from the reference program's by a relative error of at most 0.0001.
Values sent between devices are 32-bit elements; how exact they have to be, the bound alone decides.
A program may use at most 64 MiB of HBM per device.

```python
import jax
import jax.numpy as jnp
from jax import lax

W = 256
HID = 1024
HI_LAYERS = 4
LO_LAYERS = 4
POS_DEV = 256
LAYERS = 8
NPOS = 131072
N_SEQHI = 16
N_SEQLO = 32


def levels(rng, extent, pieces, least, top_value):
    level = 1.0
    for position, parts in pieces:
        steps = jax.random.uniform(jax.random.fold_in(jax.random.fold_in(rng, 6), position), (parts,), jnp.float32, least / len(pieces), top_value / len(pieces))
        level = level * jnp.repeat(jnp.exp(steps), extent[position] // parts).reshape((-1,) + (1,) * (len(extent) - 1 - position))
    return level


def gaussian(own_key, extent, width, bound, split=(), dtype=jnp.bfloat16):
    factor_of = levels(own_key, extent, split, -0.22, 0.18) if split else 1.0
    entries = jax.random.normal(own_key, extent, jnp.float32) * width * factor_of
    return jnp.minimum(jnp.maximum(entries, -bound), bound).astype(dtype)


def setup_inputs(seed: int = 0) -> dict:
    streams_of = jax.random.split(jax.random.key(seed), 7)
    return {
        "features": gaussian(streams_of[0], (NPOS, W), 1.0, 6.0, ((0, 512),), jnp.float32),
        "norm_gain": jnp.clip(1.0 + 0.18 * jax.random.normal(streams_of[1], (LAYERS, 2 * W), jnp.float32), 0.1, 1.9),
        "bias_hidden": gaussian(streams_of[2], (LAYERS, HID), 1.0, 4.0, (), jnp.float32),
        "gate_logit": jnp.clip(jax.random.uniform(streams_of[3], (LAYERS, 2 * W), jnp.float32, -2.0, 2.0), -2.0, 2.0),
        "w_in": gaussian(streams_of[4], (2 * W, HID), (2 * W) ** -0.5, 0.25, (), jnp.float32),
        "w_out": gaussian(streams_of[5], (HID, 2 * W), HID ** -0.5, 0.1875, (), jnp.float32),
    }


NORM_EPS = 1e-05

def switch_unit(lower_rows, upper_rows, layer_params):
    norm_gain, bias_hidden, gate_logit, w_in, w_out = layer_params
    feature_count = lower_rows.shape[-1]
    paired = jnp.concatenate([lower_rows, upper_rows], axis=-1)
    center = paired - lax.optimization_barrier(jnp.mean(paired, axis=-1, keepdims=True))
    spread = lax.optimization_barrier(jnp.mean(center * center, axis=-1, keepdims=True))
    normed = center * lax.rsqrt(spread + NORM_EPS) * norm_gain
    hidden = jax.nn.gelu(jnp.dot(normed, w_in, precision=lax.Precision.HIGHEST, preferred_element_type=jnp.float32) + bias_hidden)
    mixed_out = jax.nn.sigmoid(gate_logit) * paired + jnp.dot(hidden, w_out, precision=lax.Precision.HIGHEST, preferred_element_type=jnp.float32)
    return (mixed_out[:, :feature_count], mixed_out[:, feature_count:])

def pair_layer(states, distance, layer_params):
    row_count, feature_count = states.shape
    groups = row_count // (2 * distance)
    grouped = states.reshape(groups, 2, distance, feature_count)
    new_lower, new_upper = switch_unit(grouped[:, 0].reshape(-1, feature_count), grouped[:, 1].reshape(-1, feature_count), layer_params)
    joined = jnp.stack([new_lower.reshape(groups, distance, feature_count), new_upper.reshape(groups, distance, feature_count)], axis=1)
    return joined.reshape(row_count, feature_count)

def reference(features, norm_gain, bias_hidden, gate_logit, w_in, w_out):
    high_bits = N_SEQHI.bit_length() - 1
    low_bits = N_SEQLO.bit_length() - 1
    states = features
    for layer_index in range(HI_LAYERS + LO_LAYERS):
        if layer_index < HI_LAYERS:
            distance = POS_DEV * N_SEQLO * 2 ** (layer_index % high_bits)
        else:
            distance = POS_DEV * 2 ** ((layer_index - HI_LAYERS) % low_bits)
        layer_params = (norm_gain[layer_index], bias_hidden[layer_index], gate_logit[layer_index], w_in, w_out)
        states = pair_layer(states, distance, layer_params)
    return states
```

```python
import functools

import jax
import jax.numpy as jnp
from jax import lax
from jax.experimental import pallas as pl
from jax.experimental.pallas import tpu as pltpu
from jax.sharding import PartitionSpec as P

MESH = pl.DeviceIdType.MESH
BF, F32 = jnp.bfloat16, jnp.float32
NORM_EPS = 1e-05
Z, ZLO, X, Y = 16, 8, 4, 2


def ring_order(size):
    order = []
    for step in range(size):
        half = (step + 1) // 2
        order.append((size // 2 - half if step % 2 else size // 2 + half) % size)
    return order


def chips(hi, lo):
    z_lo, x, z_hi, y = lax.div(hi, 2), lax.rem(lo, 4), lax.rem(lax.div(lo, 4), 2), lax.rem(lax.div(lo, 8), 2)
    block = lo - lax.rem(lo, 16)
    z = z_hi * ZLO + z_lo
    along_x = []
    for dx in (2, 1, 3, 0):
        to = lax.rem(x + dx, X)
        along_x.append((to, lax.rem(to, 2) * 8 + lax.div(to, 2) * 4))
    along_y = [1 - y, y]
    found = []
    for dz in ring_order(Z):
        to = lax.rem(z + dz, Z)
        to_hi, to_lo = lax.div(to, ZLO), lax.rem(to, ZLO)
        place_z = lax.rem(to_lo, 2) * 64 + lax.rem(lax.div(to_lo, 2), 2) * 32 + lax.div(to_lo, 4) * 16 + to_hi * 2
        at_z = block + to_hi * 4
        for to_x, place_x in along_x:
            for to_y in along_y:
                found.append((to_lo, at_z + to_x + to_y * 8, place_z + place_x + to_y))
    return found


def halves(value):
    high = value.astype(BF)
    return high, (value - high.astype(F32)).astype(BF)


def product(value, weight_high, weight_low):
    rows = value.shape[0]
    high, low = halves(value)
    both = jnp.dot(jnp.concatenate([high, low], 0), weight_high[...], preferred_element_type=F32)
    return both[:rows] + both[rows:] + jnp.dot(high, weight_low[...], preferred_element_type=F32)


def switch(lower, upper, layer, gain, bias, gate, w_in, w_out):
    wide = lower.shape[-1]
    mean = (jnp.sum(lower, -1, keepdims=True) + jnp.sum(upper, -1, keepdims=True)) * (0.5 / wide)
    lower_c, upper_c = lower - mean, upper - mean
    spread = (jnp.sum(lower_c * lower_c, -1, keepdims=True) + jnp.sum(upper_c * upper_c, -1, keepdims=True)) * (0.5 / wide)
    scale = lax.rsqrt(spread + NORM_EPS)
    normed = jnp.concatenate([lower_c * scale, upper_c * scale], -1) * gain[pl.ds(layer, 1), :]
    hidden = jax.nn.gelu(product(normed, *w_in) + bias[pl.ds(layer, 1), :])
    out = product(hidden, *w_out)
    kept = jax.nn.sigmoid(gate[pl.ds(layer, 1), :])
    return kept[:, :wide] * lower + out[:, :wide], kept[:, wide:] * upper + out[:, wide:]


def butterfly(points, params, layers):
    rows = points.shape[1] // 2

    def step(layer, carry):
        lower = jnp.concatenate([points[0, :rows], points[1, :rows]], -1)
        upper = jnp.concatenate([points[0, rows:], points[1, rows:]], -1)
        lower, upper = switch(lower, upper, layer, *params)
        for part in range(2):
            lanes = slice(part * 128, part * 128 + 128)
            points[part, pl.ds(0, rows, stride=2), :] = lower[:, lanes]
            points[part, pl.ds(1, rows, stride=2), :] = upper[:, lanes]
        return carry

    lax.fori_loop(1, layers, step, 0)


def split_weight(whole, high, low):
    rows = whole.shape[0]

    def step(index, carry):
        at = pl.ds(pl.multiple_of(index * 64, 64), 64)
        high[at, :], low[at, :] = halves(whole[at, :])
        return carry

    lax.fori_loop(0, rows // 64, step, 0)


def took(ref, sem):
    pltpu.make_async_copy(ref, ref, sem).wait()


def kernel(
    x_hbm, gain_hbm, bias_hbm, gate_hbm, w_in_hbm, w_out_hbm, out,
    gain, bias, gate, w_in, w_out, in_high, in_low, out_high, out_low,
    away, paired, mixed, points_a, points_b, spare, loads, core_sem, in_sem, out_sem,
):
    hi, lo = lax.axis_index("seqhi"), lax.axis_index("seqlo")
    core = lax.rem(hi, 2)
    other = 1 - core
    peers = chips(hi, lo)
    my_place = peers[-1][2]
    layers = gain.shape[0]
    half = paired.shape[1]

    barrier = pltpu.get_barrier_semaphore()
    for z_lo, to_lo, _ in peers[:-1]:
        pl.semaphore_signal(barrier, inc=1, device_id=(z_lo * 2 + core, to_lo), device_id_type=MESH)
    partner = (hi + 1 - 2 * core, lo)
    pl.semaphore_signal(barrier, inc=1, device_id=partner, device_id_type=MESH)

    keep_at = pl.ds(pl.multiple_of(core * half, half), half)
    send_at = pl.ds(pl.multiple_of(other * half, half), half)
    fetched = [
        pltpu.make_async_copy(source, target, loads.at[index])
        for index, (source, target) in enumerate(
            [
                (w_in_hbm, w_in), (w_out_hbm, w_out), (gain_hbm, gain), (bias_hbm, bias), (gate_hbm, gate),
                (x_hbm.at[send_at, :], away), (x_hbm.at[keep_at, :], paired.at[core]),
            ]
        )
    ]
    for copy in fetched:
        copy.start()
    fetched[0].wait()
    split_weight(w_in, in_high, in_low)
    fetched[1].wait()
    split_weight(w_out, out_high, out_low)
    for copy in fetched[2:]:
        copy.wait()
    params = (gain, bias, gate, (in_high, in_low), (out_high, out_low))

    pl.semaphore_wait(barrier, len(peers))
    swap = pltpu.make_async_remote_copy(
        src_ref=away, dst_ref=paired.at[core], send_sem=core_sem.at[0], recv_sem=core_sem.at[1],
        device_id=partner, device_id_type=MESH,
    )
    swap.start()
    swap.wait()
    lower, upper = switch(paired[0], paired[1], 0, *params)
    for part in range(2):
        lanes = slice(part * 128, part * 128 + 128)
        mixed[0, part] = lower[:, lanes]
        mixed[1, part] = upper[:, lanes]

    for which, points in enumerate((points_a, points_b)):
        whose = core if which == 0 else other
        for z_lo, to_lo, place in peers[:-1]:
            pltpu.make_async_remote_copy(
                src_ref=mixed.at[whose, :, pl.ds(place, 1), :], dst_ref=points.at[:, pl.ds(my_place, 1), :],
                send_sem=in_sem.at[0, which], recv_sem=in_sem.at[1, which],
                device_id=(z_lo * 2 + core, to_lo), device_id_type=MESH,
            ).start()
        own = mixed.at[whose, :, pl.ds(my_place, 1), :]
        pltpu.make_async_copy(own, points.at[:, pl.ds(my_place, 1), :], in_sem.at[1, which]).start()
        pltpu.make_async_copy(own, spare.at[which, :, pl.ds(0, 1), :], in_sem.at[0, which]).start()

    home = pl.ds(core * half + my_place, 1)
    for which, points in enumerate((points_a, points_b)):
        whose = core if which == 0 else other
        took(points, in_sem.at[1, which])
        butterfly(points, params, layers)
        for z_lo, to_lo, place in peers[: len(peers) - 1 + which]:
            for part in range(2):
                pltpu.make_async_remote_copy(
                    src_ref=points.at[part, pl.ds(place, 1), :], dst_ref=out.at[home, pl.ds(part * 128, 128)],
                    send_sem=out_sem.at[0, which], recv_sem=out_sem.at[1, which],
                    device_id=(z_lo * 2 + whose, to_lo), device_id_type=MESH,
                ).start()
        if which == 0:
            for part in range(2):
                own = points.at[part, pl.ds(my_place, 1), :]
                pltpu.make_async_copy(own, out.at[home, pl.ds(part * 128, 128)], out_sem.at[1, which]).start()
                pltpu.make_async_copy(own, spare.at[2, part, pl.ds(0, 1), :], out_sem.at[0, which]).start()

    for which, points in enumerate((points_a, points_b)):
        took(points, in_sem.at[0, which])
        took(points, out_sem.at[0, which])
    took(out.at[keep_at, :], out_sem.at[1, 0])
    took(out.at[send_at, :], out_sem.at[1, 1])


def body(features, norm_gain, bias_hidden, gate_logit, w_in, w_out):
    rows, wide = features.shape
    half = rows // 2
    anywhere = pl.BlockSpec(memory_space=pltpu.HBM)
    sem = pltpu.SemaphoreType.DMA
    vmem = lambda dtype, *shape: pltpu.VMEM(shape, dtype)
    return pl.pallas_call(
        kernel,
        out_shape=jax.ShapeDtypeStruct((rows, wide), F32),
        in_specs=[anywhere] * 6,
        out_specs=pl.BlockSpec(memory_space=pltpu.VMEM),
        scratch_shapes=[
            vmem(F32, *norm_gain.shape), vmem(F32, *bias_hidden.shape), vmem(F32, *gate_logit.shape),
            vmem(F32, *w_in.shape), vmem(F32, *w_out.shape),
            vmem(BF, *w_in.shape), vmem(BF, *w_in.shape), vmem(BF, *w_out.shape), vmem(BF, *w_out.shape),
            vmem(F32, half, wide), vmem(F32, 2, half, wide), vmem(F32, 2, 2, half, 128),
            vmem(F32, 2, half, 128), vmem(F32, 2, half, 128), vmem(F32, 3, 2, 8, 128),
            sem((7,)), sem((2,)), sem((2, 2)), sem((2, 2)),
        ],
        compiler_params=pltpu.CompilerParams(collective_id=0, has_side_effects=True, vmem_limit_bytes=48 << 20),
    )(features, norm_gain, bias_hidden, gate_logit, w_in, w_out)


def solution(mesh):
    placed = (P(("seqhi", "seqlo"), None), P(), P(), P(), P(), P())
    return jax.shard_map(body, mesh=mesh, in_specs=placed, out_specs=P(("seqhi", "seqlo"), None), check_vma=False)
```

```python
import math

import jax
import jax.numpy as jnp
from jax import lax
from jax.experimental import pallas as pl
from jax.experimental.pallas import tpu as pltpu
from jax.sharding import PartitionSpec as P

MESH = pl.DeviceIdType.MESH
BF, F32 = jnp.bfloat16, jnp.float32
NORM_EPS = 1e-05
GELU_A = (2 / math.pi) ** 0.5
GELU_B = GELU_A * 0.044715
Z, ZLO, X, Y = 16, 8, 4, 2


def ring_order(size):
    order = []
    for step in range(size):
        half = (step + 1) // 2
        order.append((size // 2 - half if step % 2 else size // 2 + half) % size)
    return order


def chips(hi, lo):
    z_lo, x, z_hi, y = lax.div(hi, 2), lax.rem(lo, 4), lax.rem(lax.div(lo, 4), 2), lax.rem(lax.div(lo, 8), 2)
    block = lo - lax.rem(lo, 16)
    z = z_hi * ZLO + z_lo
    along_x = []
    for dx in (2, 1, 3, 0):
        to = lax.rem(x + dx, X)
        along_x.append((to, lax.rem(to, 2) * 8 + lax.div(to, 2) * 4))
    along_y = [1 - y, y]
    found = []
    for dz in ring_order(Z):
        to = lax.rem(z + dz, Z)
        to_hi, to_lo = lax.div(to, ZLO), lax.rem(to, ZLO)
        place_z = lax.rem(to_lo, 2) * 64 + lax.rem(lax.div(to_lo, 2), 2) * 32 + lax.div(to_lo, 4) * 16 + to_hi * 2
        at_z = block + to_hi * 4
        for to_x, place_x in along_x:
            for to_y in along_y:
                found.append((to_lo, at_z + to_x + to_y * 8, place_z + place_x + to_y))
    return found


def gelu(value):
    inner = value * (GELU_A + GELU_B * (value * value))
    half = 0.5 * value
    return half + half * jnp.tanh(inner)


def halves(value):
    high = value.astype(BF)
    return high, (value - high.astype(F32)).astype(BF)


def product(value, weight_high, weight_low):
    rows = value.shape[0]
    high, low = halves(value)
    stacked = jnp.concatenate([high, low], 0)
    columns = []
    for block in range(0, weight_high.shape[0], 2):
        tile_high = jnp.concatenate([weight_high[block], weight_high[block + 1]], -1)
        tile_low = jnp.concatenate([weight_low[block], weight_low[block + 1]], -1)
        both = jnp.dot(stacked, tile_high, preferred_element_type=F32)
        columns.append(both[:rows] + both[rows:] + jnp.dot(high, tile_low, preferred_element_type=F32))
    return jnp.concatenate(columns, -1)


def switch(lower, upper, layer, gain, bias, gate, w_in, w_out):
    wide = lower.shape[-1]
    mean = (jnp.sum(lower, -1, keepdims=True) + jnp.sum(upper, -1, keepdims=True)) * (0.5 / wide)
    lower_c, upper_c = lower - mean, upper - mean
    spread = (jnp.sum(lower_c * lower_c, -1, keepdims=True) + jnp.sum(upper_c * upper_c, -1, keepdims=True)) * (0.5 / wide)
    scale = lax.rsqrt(spread + NORM_EPS)
    normed = jnp.concatenate([lower_c * scale, upper_c * scale], -1) * gain[pl.ds(layer, 1), :]
    hidden = gelu(product(normed, *w_in) + bias[pl.ds(layer, 1), :])
    out = product(hidden, *w_out)
    kept = jax.nn.sigmoid(gate[pl.ds(layer, 1), :])
    return kept[:, :wide] * lower + out[:, :wide], kept[:, wide:] * upper + out[:, wide:]


def butterfly(points, params, layers):
    rows = points.shape[1] // 2

    def step(layer, carry):
        lower = jnp.concatenate([points[0, :rows], points[1, :rows]], -1)
        upper = jnp.concatenate([points[0, rows:], points[1, rows:]], -1)
        lower, upper = switch(lower, upper, layer, *params)
        for part in range(2):
            lanes = slice(part * 128, part * 128 + 128)
            points[part, pl.ds(0, rows, stride=2), :] = lower[:, lanes]
            points[part, pl.ds(1, rows, stride=2), :] = upper[:, lanes]
        return carry

    lax.fori_loop(1, layers, step, 0)


def split_weight(whole, high, low):
    rows = whole.shape[0]

    def step(index, carry):
        at = pl.ds(pl.multiple_of(index * 64, 64), 64)
        for block in range(high.shape[0]):
            high[block, at, :], low[block, at, :] = halves(whole[at, block * 128 : block * 128 + 128])
        return carry

    lax.fori_loop(0, rows // 64, step, 0)


def took(ref, sem):
    pltpu.make_async_copy(ref, ref, sem).wait()


def kernel(
    x_hbm, gain_hbm, bias_hbm, gate_hbm, w_in_hbm, w_out_hbm, out,
    gain, bias, gate, w_in, w_out, in_high, in_low, out_high, out_low,
    away, paired, mixed, points_a, points_b, arrived, spare, loads, core_sem, in_sem, out_sem,
):
    hi, lo = lax.axis_index("seqhi"), lax.axis_index("seqlo")
    core = lax.rem(hi, 2)
    other = 1 - core
    peers = chips(hi, lo)
    my_place = peers[-1][2]
    layers = gain.shape[0]
    half = paired.shape[1]

    barrier = pltpu.get_barrier_semaphore()
    for z_lo, to_lo, _ in peers[:-1]:
        pl.semaphore_signal(barrier, inc=1, device_id=(z_lo * 2 + core, to_lo), device_id_type=MESH)
    partner = (hi + 1 - 2 * core, lo)
    pl.semaphore_signal(barrier, inc=1, device_id=partner, device_id_type=MESH)

    keep_at = pl.ds(pl.multiple_of(core * half, half), half)
    send_at = pl.ds(pl.multiple_of(other * half, half), half)
    fetched = [
        pltpu.make_async_copy(source, target, loads.at[index])
        for index, (source, target) in enumerate(
            [
                (w_in_hbm, w_in), (w_out_hbm, w_out), (gain_hbm, gain), (bias_hbm, bias), (gate_hbm, gate),
                (x_hbm.at[send_at, :], away), (x_hbm.at[keep_at, :], paired.at[core]),
            ]
        )
    ]
    for copy in fetched:
        copy.start()
    fetched[0].wait()
    split_weight(w_in, in_high, in_low)
    fetched[1].wait()
    split_weight(w_out, out_high, out_low)
    for copy in fetched[2:]:
        copy.wait()
    params = (gain, bias, gate, (in_high, in_low), (out_high, out_low))

    pl.semaphore_wait(barrier, len(peers))
    swap = pltpu.make_async_remote_copy(
        src_ref=away, dst_ref=paired.at[core], send_sem=core_sem.at[0], recv_sem=core_sem.at[1],
        device_id=partner, device_id_type=MESH,
    )
    swap.start()
    swap.wait()
    lower, upper = switch(paired[0], paired[1], 0, *params)
    for part in range(2):
        lanes = slice(part * 128, part * 128 + 128)
        mixed[0, part] = lower[:, lanes]
        mixed[1, part] = upper[:, lanes]

    for which, points in enumerate((points_a, points_b)):
        whose = core if which == 0 else other
        for z_lo, to_lo, place in peers[:-1]:
            pltpu.make_async_remote_copy(
                src_ref=mixed.at[whose, :, pl.ds(place, 1), :], dst_ref=points.at[:, pl.ds(my_place, 1), :],
                send_sem=in_sem.at[0, which], recv_sem=in_sem.at[1, which],
                device_id=(z_lo * 2 + core, to_lo), device_id_type=MESH,
            ).start()
        own = mixed.at[whose, :, pl.ds(my_place, 1), :]
        pltpu.make_async_copy(own, points.at[:, pl.ds(my_place, 1), :], in_sem.at[1, which]).start()
        pltpu.make_async_copy(own, spare.at[which, :, pl.ds(0, 1), :], in_sem.at[0, which]).start()

    home = pl.ds(core * half + my_place, 1)
    for which, points in enumerate((points_a, points_b)):
        whose = core if which == 0 else other
        took(points, in_sem.at[1, which])
        butterfly(points, params, layers)
        for z_lo, to_lo, place in peers[: len(peers) - 1 + which]:
            pltpu.make_async_remote_copy(
                src_ref=points.at[:, pl.ds(place, 1), :], dst_ref=arrived.at[:, home, :],
                send_sem=out_sem.at[0, which], recv_sem=out_sem.at[1, which],
                device_id=(z_lo * 2 + whose, to_lo), device_id_type=MESH,
            ).start()
        if which == 0:
            own = points.at[:, pl.ds(my_place, 1), :]
            pltpu.make_async_copy(own, arrived.at[:, home, :], out_sem.at[1, which]).start()
            pltpu.make_async_copy(own, spare.at[2, :, pl.ds(0, 1), :], out_sem.at[0, which]).start()

    for which, points in enumerate((points_a, points_b)):
        took(points, in_sem.at[0, which])
        took(points, out_sem.at[0, which])
    took(arrived.at[:, keep_at, :], out_sem.at[1, 0])
    took(arrived.at[:, send_at, :], out_sem.at[1, 1])
    for part in range(2):
        out[:, part * 128 : part * 128 + 128] = arrived[part]


def body(features, norm_gain, bias_hidden, gate_logit, w_in, w_out):
    rows, wide = features.shape
    half = rows // 2
    anywhere = pl.BlockSpec(memory_space=pltpu.HBM)
    sem = pltpu.SemaphoreType.DMA
    vmem = lambda dtype, *shape: pltpu.VMEM(shape, dtype)
    return pl.pallas_call(
        kernel,
        out_shape=jax.ShapeDtypeStruct((rows, wide), F32),
        in_specs=[anywhere] * 6,
        out_specs=pl.BlockSpec(memory_space=pltpu.VMEM),
        scratch_shapes=[
            vmem(F32, *norm_gain.shape), vmem(F32, *bias_hidden.shape), vmem(F32, *gate_logit.shape),
            vmem(F32, *w_in.shape), vmem(F32, *w_out.shape),
            *[vmem(BF, w.shape[1] // 128, w.shape[0], 128) for w in (w_in, w_in, w_out, w_out)],
            vmem(F32, half, wide), vmem(F32, 2, half, wide), vmem(F32, 2, 2, half, 128),
            vmem(F32, 2, half, 128), vmem(F32, 2, half, 128), vmem(F32, 2, rows, 128), vmem(F32, 3, 2, 8, 128),
            sem((7,)), sem((2,)), sem((2, 2)), sem((2, 2)),
        ],
        compiler_params=pltpu.CompilerParams(collective_id=0, has_side_effects=True, vmem_limit_bytes=40 << 20),
    )(*[pltpu.with_memory_space_constraint(a, pltpu.HBM) for a in (features, norm_gain, bias_hidden, gate_logit, w_in, w_out)])


def solution(mesh):
    placed = (P(("seqhi", "seqlo"), None), P(), P(), P(), P(), P())
    return jax.shard_map(body, mesh=mesh, in_specs=placed, out_specs=P(("seqhi", "seqlo"), None), check_vma=False)
```

```python
import math

import jax
import jax.numpy as jnp
from jax import lax
from jax.experimental import pallas as pl
from jax.experimental.pallas import tpu as pltpu
from jax.sharding import PartitionSpec as P

MESH = pl.DeviceIdType.MESH
BF, F32 = jnp.bfloat16, jnp.float32
NORM_EPS = 1e-05
GELU_A = (2 / math.pi) ** 0.5
GELU_B = GELU_A * 0.044715
Z, ZLO, X, Y = 16, 8, 4, 2


def ring_order(size):
    order = []
    for step in range(size):
        half = (step + 1) // 2
        order.append((size // 2 - half if step % 2 else size // 2 + half) % size)
    return order


def chips(hi, lo, turns_z, at_y=None):
    z_lo, x, z_hi, y = lax.div(hi, 2), lax.rem(lo, 4), lax.rem(lax.div(lo, 4), 2), lax.rem(lax.div(lo, 8), 2)
    block = lo - lax.rem(lo, 16)
    z = z_hi * ZLO + z_lo
    along_x = []
    for dx in (2, 1, 3, 0):
        to = lax.rem(x + dx, X)
        along_x.append((to, lax.rem(to, 2) * 8 + lax.div(to, 2) * 4))
    along_y = [1 - y, y] if at_y is None else at_y
    found = []
    for dz in turns_z:
        to = lax.rem(z + dz, Z)
        to_hi, to_lo = lax.div(to, ZLO), lax.rem(to, ZLO)
        place_z = lax.rem(to_lo, 2) * 64 + lax.rem(lax.div(to_lo, 2), 2) * 32 + lax.div(to_lo, 4) * 16 + to_hi * 2
        at_z = block + to_hi * 4
        for to_x, place_x in along_x:
            for to_y in along_y:
                found.append((to_lo, at_z + to_x + to_y * 8, place_z + place_x + to_y))
    return found


def gelu(value):
    inner = value * (GELU_A + GELU_B * (value * value))
    half = 0.5 * value
    return half + half * jnp.tanh(inner)


def halves(value):
    high = value.astype(BF)
    return high, (value - high.astype(F32)).astype(BF)


def product(value, weight_high, weight_low, beside):
    rows = value.shape[0]
    high, low = halves(value)
    stacked = jnp.concatenate([high, low], 0)
    columns = []
    for block in range(0, weight_high.shape[0], 2):
        tile_high = jnp.concatenate([weight_high[block], weight_high[block + 1]], -1)
        tile_low = jnp.concatenate([weight_low[block], weight_low[block + 1]], -1)
        both = jnp.dot(stacked, tile_high, preferred_element_type=F32)
        columns.append(both[:rows] + both[rows:] + jnp.dot(high, tile_low, preferred_element_type=F32))
        beside(columns)
    return jnp.concatenate(columns, -1)


def switch(lower, upper, layer, params, done, beside=lambda columns: None):
    gain, bias, gate, w_in, w_out = params
    wide = lower.shape[-1]
    mean = (jnp.sum(lower, -1, keepdims=True) + jnp.sum(upper, -1, keepdims=True)) * (0.5 / wide)
    lower_c, upper_c = lower - mean, upper - mean
    spread = (jnp.sum(lower_c * lower_c, -1, keepdims=True) + jnp.sum(upper_c * upper_c, -1, keepdims=True)) * (0.5 / wide)
    scale = lax.rsqrt(spread + NORM_EPS)
    normed = jnp.concatenate([lower_c * scale, upper_c * scale], -1) * gain[pl.ds(layer, 1), :]
    hidden = gelu(product(normed, *w_in, beside) + bias[pl.ds(layer, 1), :])
    kept = jax.nn.sigmoid(gate[pl.ds(layer, 1), :])

    def finish(columns):
        side = len(columns) - 1
        old = (lower, upper)[side]
        done(side, kept[:, side * wide : side * wide + wide] * old + columns[side])

    product(hidden, *w_out, finish)


def pair_layer(points, layer, params, beside=lambda columns: None, after=lambda side: None):
    rows = points.shape[0] // 4
    lower = jnp.concatenate([points[pl.ds(part, rows, stride=2), :] for part in range(2)], -1)
    upper = jnp.concatenate([points[pl.ds(2 * rows + part, rows, stride=2), :] for part in range(2)], -1)

    def done(side, value):
        for part in range(2):
            points[pl.ds(2 * side + part, rows, stride=4), :] = value[:, part * 128 : part * 128 + 128]
        after(side)

    switch(lower, upper, layer, params, done, beside)


def split_weight(whole, high, low):
    rows = whole.shape[0]

    def step(index, carry):
        at = pl.ds(pl.multiple_of(index * 64, 64), 64)
        for block in range(high.shape[0]):
            high[block, at, :], low[block, at, :] = halves(whole[at, block * 128 : block * 128 + 128])
        return carry

    lax.fori_loop(0, rows // 64, step, 0)


def row_at(place):
    return pl.ds(pl.multiple_of(2 * place, 2), 2)


def took(ref, sem):
    pltpu.make_async_copy(ref, ref, sem).wait()


def kernel(
    x_hbm, gain_hbm, bias_hbm, gate_hbm, w_in_hbm, w_out_hbm, out,
    gain, bias, gate, w_in, w_out, in_high, in_low, out_high, out_low,
    away, paired, mixed, points_a, points_b, arrived, spare, loads, core_sem, in_sem, out_sem,
):
    hi, lo = lax.axis_index("seqhi"), lax.axis_index("seqlo")
    core = lax.rem(hi, 2)
    other = 1 - core
    peers = chips(hi, lo, ring_order(Z))
    my_place = peers[-1][2]
    layers = gain.shape[0]
    half = paired.shape[1]

    barrier = pltpu.get_barrier_semaphore()
    for z_lo, to_lo, _ in peers[:-1]:
        pl.semaphore_signal(barrier, inc=1, device_id=(z_lo * 2 + core, to_lo), device_id_type=MESH)
    partner = (hi + 1 - 2 * core, lo)
    pl.semaphore_signal(barrier, inc=1, device_id=partner, device_id_type=MESH)

    keep_at = pl.ds(pl.multiple_of(core * half, half), half)
    send_at = pl.ds(pl.multiple_of(other * half, half), half)
    fetched = [
        pltpu.make_async_copy(source, target, loads.at[index])
        for index, (source, target) in enumerate(
            [
                (w_in_hbm, w_in), (w_out_hbm, w_out), (gain_hbm, gain), (bias_hbm, bias), (gate_hbm, gate),
                (x_hbm.at[send_at, :], away), (x_hbm.at[keep_at, :], paired.at[core]),
            ]
        )
    ]
    for copy in fetched:
        copy.start()
    fetched[0].wait()
    split_weight(w_in, in_high, in_low)
    fetched[1].wait()
    split_weight(w_out, out_high, out_low)
    for copy in fetched[2:]:
        copy.wait()
    params = (gain, bias, gate, (in_high, in_low), (out_high, out_low))

    pl.semaphore_wait(barrier, len(peers))
    swap = pltpu.make_async_remote_copy(
        src_ref=away, dst_ref=paired.at[core], send_sem=core_sem.at[0], recv_sem=core_sem.at[1],
        device_id=partner, device_id_type=MESH,
    )
    swap.start()
    swap.wait()

    def mix(side, value):
        for part in range(2):
            mixed[side, pl.ds(part, half, stride=2), :] = value[:, part * 128 : part * 128 + 128]

    switch(paired[0], paired[1], 0, params, mix)

    for which, points in enumerate((points_a, points_b)):
        whose = core if which == 0 else other
        for z_lo, to_lo, place in peers[:-1]:
            pltpu.make_async_remote_copy(
                src_ref=mixed.at[whose, row_at(place), :], dst_ref=points.at[row_at(my_place), :],
                send_sem=in_sem.at[0, which], recv_sem=in_sem.at[1, which],
                device_id=(z_lo * 2 + core, to_lo), device_id_type=MESH,
            ).start()
        own = mixed.at[whose, row_at(my_place), :]
        pltpu.make_async_copy(own, points.at[row_at(my_place), :], in_sem.at[1, which]).start()
        pltpu.make_async_copy(own, spare.at[which, pl.ds(0, 2), :], in_sem.at[0, which]).start()

    home = row_at(core * half + my_place)

    def send_home(which, points, peer):
        z_lo, to_lo, place = peer
        pltpu.make_async_remote_copy(
            src_ref=points.at[row_at(place), :], dst_ref=arrived.at[home, :],
            send_sem=out_sem.at[0, which], recv_sem=out_sem.at[1, which],
            device_id=(z_lo * 2 + (core if which == 0 else other), to_lo), device_id_type=MESH,
        ).start()

    took(points_a, in_sem.at[1, 0])

    def alone(layer, carry):
        pair_layer(points_a, layer, params)
        return carry

    lax.fori_loop(1, layers, alone, 0)
    own = points_a.at[row_at(my_place), :]
    pltpu.make_async_copy(own, arrived.at[home, :], out_sem.at[1, 0]).start()
    pltpu.make_async_copy(own, spare.at[2, pl.ds(0, 2), :], out_sem.at[0, 0]).start()
    for peer in chips(hi, lo, (Z - 1, 0))[:-1]:
        send_home(0, points_a, peer)
    took(points_b, in_sem.at[1, 1])

    def both(layer, carry):
        waiting = chips(hi, lo, (Z // 2 - 1 + layer, Z // 2 - layer))
        share = len(waiting) // 4

        def send_some(columns):
            for peer in waiting[len(columns) * share - share : len(columns) * share]:
                send_home(0, points_a, peer)

        pair_layer(points_b, layer, params, send_some)
        return carry

    lax.fori_loop(1, layers - 1, both, 0)
    by_y = [chips(hi, lo, ring_order(Z), (side,)) for side in range(2)]
    last = chips(hi, lo, (Z - 2, 1))

    def send_last(columns):
        for peer in last[len(columns) * 4 - 4 : len(columns) * 4]:
            send_home(0, points_a, peer)

    def leave(side):
        for peer in by_y[side]:
            send_home(1, points_b, peer)

    pair_layer(points_b, layers - 1, params, send_last, leave)

    for which, points in enumerate((points_a, points_b)):
        took(points, in_sem.at[0, which])
        took(points, out_sem.at[0, which])
    took(arrived.at[pl.ds(0, 2 * half), :], out_sem.at[1, 0])
    took(arrived.at[pl.ds(0, 2 * half), :], out_sem.at[1, 1])
    for part in range(2):
        out[:, part * 128 : part * 128 + 128] = arrived[pl.ds(part, 2 * half, stride=2), :]


def body(features, norm_gain, bias_hidden, gate_logit, w_in, w_out):
    rows, wide = features.shape
    half = rows // 2
    anywhere = pl.BlockSpec(memory_space=pltpu.HBM)
    sem = pltpu.SemaphoreType.DMA
    vmem = lambda dtype, *shape: pltpu.VMEM(shape, dtype)
    return pl.pallas_call(
        kernel,
        out_shape=jax.ShapeDtypeStruct((rows, wide), F32),
        in_specs=[anywhere] * 6,
        out_specs=pl.BlockSpec(memory_space=pltpu.VMEM),
        scratch_shapes=[
            vmem(F32, *norm_gain.shape), vmem(F32, *bias_hidden.shape), vmem(F32, *gate_logit.shape),
            vmem(F32, *w_in.shape), vmem(F32, *w_out.shape),
            *[vmem(BF, w.shape[1] // 128, w.shape[0], 128) for w in (w_in, w_in, w_out, w_out)],
            vmem(F32, half, wide), vmem(F32, 2, half, wide), vmem(F32, 2, 2 * half, 128),
            vmem(F32, 2 * half, 128), vmem(F32, 2 * half, 128), vmem(F32, 2 * rows, 128), vmem(F32, 3, 8, 128),
            sem((7,)), sem((2,)), sem((2, 2)), sem((2, 2)),
        ],
        compiler_params=pltpu.CompilerParams(collective_id=0, has_side_effects=True, vmem_limit_bytes=40 << 20),
    )(*[pltpu.with_memory_space_constraint(a, pltpu.HBM) for a in (features, norm_gain, bias_hidden, gate_logit, w_in, w_out)])


def solution(mesh):
    placed = (P(("seqhi", "seqlo"), None), P(), P(), P(), P(), P())
    return jax.shard_map(body, mesh=mesh, in_specs=placed, out_specs=P(("seqhi", "seqlo"), None), check_vma=False)
```

```python
import math

import jax
import jax.numpy as jnp
from jax import lax
from jax.experimental import pallas as pl
from jax.experimental.pallas import tpu as pltpu
from jax.sharding import PartitionSpec as P

MESH = pl.DeviceIdType.MESH
BF, F32 = jnp.bfloat16, jnp.float32
NORM_EPS = 1e-05
GELU_A = (2 / math.pi) ** 0.5
GELU_B = GELU_A * 0.044715
Z, ZLO, X = 16, 8, 4
SHARED = 2


def ring_order(size):
    order = []
    for step in range(size):
        half = (step + 1) // 2
        order.append((size // 2 - half if step % 2 else size // 2 + half) % size)
    return order


def chips(hi, lo, turns_z, at_y=None):
    z_lo, x, z_hi, y = lax.div(hi, 2), lax.rem(lo, 4), lax.rem(lax.div(lo, 4), 2), lax.rem(lax.div(lo, 8), 2)
    block = lo - lax.rem(lo, 16)
    z = z_hi * ZLO + z_lo
    along_x = []
    for dx in (2, 1, 3, 0):
        to = lax.rem(x + dx, X)
        along_x.append((to, lax.rem(to, 2) * 8 + lax.div(to, 2) * 4))
    along_y = [1 - y, y] if at_y is None else at_y
    found = []
    for dz in turns_z:
        to = lax.rem(z + dz, Z)
        to_hi, to_lo = lax.div(to, ZLO), lax.rem(to, ZLO)
        place_z = lax.rem(to_lo, 2) * 64 + lax.rem(lax.div(to_lo, 2), 2) * 32 + lax.div(to_lo, 4) * 16 + to_hi * 2
        at_z = block + to_hi * 4
        for to_x, place_x in along_x:
            for to_y in along_y:
                found.append((to_lo, at_z + to_x + to_y * 8, place_z + place_x + to_y))
    return found


def gelu(value):
    inner = value * (GELU_A + GELU_B * (value * value))
    half = 0.5 * value
    return half + half * jnp.tanh(inner)


def halves(value):
    high = value.astype(BF)
    return high, (value - high.astype(F32)).astype(BF)


def product(value, weight_high, weight_low, beside=lambda columns: None):
    rows = value.shape[0]
    high, low = halves(value)
    stacked = jnp.concatenate([high, low], 0)
    columns = []
    for block in range(0, weight_high.shape[0], 2):
        tile_high = jnp.concatenate([weight_high[block], weight_high[block + 1]], -1)
        tile_low = jnp.concatenate([weight_low[block], weight_low[block + 1]], -1)
        both = jnp.dot(stacked, tile_high, preferred_element_type=F32)
        columns.append(both[:rows] + both[rows:] + jnp.dot(high, tile_low, preferred_element_type=F32))
        beside(columns)
    return jnp.concatenate(columns, -1)


def switch(pairs, params, done):
    gain, bias, gate, w_in, w_out = params
    wide = pairs[0][0].shape[-1]
    rows = pairs[0][0].shape[0]
    normed = []
    for lower, upper, layer in pairs:
        mean = (jnp.sum(lower, -1, keepdims=True) + jnp.sum(upper, -1, keepdims=True)) * (0.5 / wide)
        lower_c, upper_c = lower - mean, upper - mean
        spread = (jnp.sum(lower_c * lower_c, -1, keepdims=True) + jnp.sum(upper_c * upper_c, -1, keepdims=True)) * (0.5 / wide)
        scale = lax.rsqrt(spread + NORM_EPS)
        normed.append(jnp.concatenate([lower_c * scale, upper_c * scale], -1) * gain[pl.ds(layer, 1), :])
    inner = product(jnp.concatenate(normed, 0), *w_in)
    hidden = [gelu(inner[i * rows : i * rows + rows] + bias[pl.ds(layer, 1), :]) for i, (_, _, layer) in enumerate(pairs)]
    kept = [jax.nn.sigmoid(gate[pl.ds(layer, 1), :]) for _, _, layer in pairs]

    def finish(columns):
        side = len(columns) - 1
        for i, pair in enumerate(pairs):
            done(i, side, kept[i][:, side * wide : side * wide + wide] * pair[side] + columns[side][i * rows : i * rows + rows])

    product(jnp.concatenate(hidden, 0), *w_out, finish)


def pair_layers(instances, params, after=lambda side: None):
    pairs = []
    for points, layer in instances:
        rows = points.shape[0] // 4
        lower = jnp.concatenate([points[pl.ds(part, rows, stride=2), :] for part in range(2)], -1)
        upper = jnp.concatenate([points[pl.ds(2 * rows + part, rows, stride=2), :] for part in range(2)], -1)
        pairs.append((lower, upper, layer))

    def done(i, side, value):
        points = instances[i][0]
        for part in range(2):
            points[pl.ds(2 * side + part, rows, stride=4), :] = value[:, part * 128 : part * 128 + 128]
        if i == len(pairs) - 1:
            after(side)

    switch(pairs, params, done)


def split_weight(whole, high, low):
    rows = whole.shape[0]

    def step(index, carry):
        at = pl.ds(pl.multiple_of(index * 64, 64), 64)
        for block in range(high.shape[0]):
            high[block, at, :], low[block, at, :] = halves(whole[at, block * 128 : block * 128 + 128])
        return carry

    lax.fori_loop(0, rows // 64, step, 0)


def row_at(place):
    return pl.ds(pl.multiple_of(2 * place, 2), 2)


def took(ref, sem):
    pltpu.make_async_copy(ref, ref, sem).wait()


def kernel(
    x_hbm, gain_hbm, bias_hbm, gate_hbm, w_in_hbm, w_out_hbm, out,
    gain, bias, gate, w_in, w_out, in_high, in_low, out_high, out_low,
    away, paired, mixed, points_a, points_b, arrived, spare, loads, core_sem, in_sem, out_sem,
):
    hi, lo = lax.axis_index("seqhi"), lax.axis_index("seqlo")
    core = lax.rem(hi, 2)
    other = 1 - core
    peers = chips(hi, lo, ring_order(Z))
    my_place = peers[-1][2]
    layers = gain.shape[0]
    half = paired.shape[1]

    barrier = pltpu.get_barrier_semaphore()
    for z_lo, to_lo, _ in peers[:-1]:
        pl.semaphore_signal(barrier, inc=1, device_id=(z_lo * 2 + core, to_lo), device_id_type=MESH)
    partner = (hi + 1 - 2 * core, lo)
    pl.semaphore_signal(barrier, inc=1, device_id=partner, device_id_type=MESH)

    keep_at = pl.ds(pl.multiple_of(core * half, half), half)
    send_at = pl.ds(pl.multiple_of(other * half, half), half)
    fetched = [
        pltpu.make_async_copy(source, target, loads.at[index])
        for index, (source, target) in enumerate(
            [
                (w_in_hbm, w_in), (w_out_hbm, w_out), (gain_hbm, gain), (bias_hbm, bias), (gate_hbm, gate),
                (x_hbm.at[send_at, :], away), (x_hbm.at[keep_at, :], paired.at[core]),
            ]
        )
    ]
    for copy in fetched:
        copy.start()
    fetched[0].wait()
    split_weight(w_in, in_high, in_low)
    fetched[1].wait()
    split_weight(w_out, out_high, out_low)
    for copy in fetched[2:]:
        copy.wait()
    params = (gain, bias, gate, (in_high, in_low), (out_high, out_low))

    pl.semaphore_wait(barrier, len(peers))
    swap = pltpu.make_async_remote_copy(
        src_ref=away, dst_ref=paired.at[core], send_sem=core_sem.at[0], recv_sem=core_sem.at[1],
        device_id=partner, device_id_type=MESH,
    )
    swap.start()
    swap.wait()

    def mix(_, side, value):
        for part in range(2):
            mixed[side, pl.ds(part, half, stride=2), :] = value[:, part * 128 : part * 128 + 128]

    switch([(paired[0], paired[1], 0)], params, mix)

    for which, points in enumerate((points_a, points_b)):
        whose = core if which == 0 else other
        for z_lo, to_lo, place in peers[:-1]:
            pltpu.make_async_remote_copy(
                src_ref=mixed.at[whose, row_at(place), :], dst_ref=points.at[row_at(my_place), :],
                send_sem=in_sem.at[0, which], recv_sem=in_sem.at[1, which],
                device_id=(z_lo * 2 + core, to_lo), device_id_type=MESH,
            ).start()
        own = mixed.at[whose, row_at(my_place), :]
        pltpu.make_async_copy(own, points.at[row_at(my_place), :], in_sem.at[1, which]).start()
        pltpu.make_async_copy(own, spare.at[which, pl.ds(0, 2), :], in_sem.at[0, which]).start()

    home = row_at(core * half + my_place)

    def send_home(which, points, peer):
        z_lo, to_lo, place = peer
        pltpu.make_async_remote_copy(
            src_ref=points.at[row_at(place), :], dst_ref=arrived.at[home, :],
            send_sem=out_sem.at[0, which], recv_sem=out_sem.at[1, which],
            device_id=(z_lo * 2 + (core if which == 0 else other), to_lo), device_id_type=MESH,
        ).start()

    took(points_a, in_sem.at[1, 0])

    def alone(points, first, end):
        def step(layer, carry):
            pair_layers([(points, layer)], params)
            return carry

        lax.fori_loop(first, end, step, 0)

    def together(layer, carry):
        pair_layers([(points_a, layer), (points_b, layer + SHARED + 1 - layers)], params)
        return carry

    alone(points_a, 1, layers - SHARED)
    took(points_b, in_sem.at[1, 1])
    lax.fori_loop(layers - SHARED, layers, together, 0)
    own = points_a.at[row_at(my_place), :]
    pltpu.make_async_copy(own, arrived.at[home, :], out_sem.at[1, 0]).start()
    pltpu.make_async_copy(own, spare.at[2, pl.ds(0, 2), :], out_sem.at[0, 0]).start()
    for peer in peers[:-1]:
        send_home(0, points_a, peer)
    alone(points_b, SHARED + 1, layers - 1)
    by_y = [chips(hi, lo, ring_order(Z), (side,)) for side in range(2)]

    def leave(side):
        for peer in by_y[side]:
            send_home(1, points_b, peer)

    pair_layers([(points_b, layers - 1)], params, leave)

    for which, points in enumerate((points_a, points_b)):
        took(points, in_sem.at[0, which])
        took(points, out_sem.at[0, which])
    took(arrived.at[pl.ds(0, 2 * half), :], out_sem.at[1, 0])
    took(arrived.at[pl.ds(0, 2 * half), :], out_sem.at[1, 1])
    for part in range(2):
        out[:, part * 128 : part * 128 + 128] = arrived[pl.ds(part, 2 * half, stride=2), :]


def body(features, norm_gain, bias_hidden, gate_logit, w_in, w_out):
    rows, wide = features.shape
    half = rows // 2
    anywhere = pl.BlockSpec(memory_space=pltpu.HBM)
    sem = pltpu.SemaphoreType.DMA
    vmem = lambda dtype, *shape: pltpu.VMEM(shape, dtype)
    return pl.pallas_call(
        kernel,
        out_shape=jax.ShapeDtypeStruct((rows, wide), F32),
        in_specs=[anywhere] * 6,
        out_specs=pl.BlockSpec(memory_space=pltpu.VMEM),
        scratch_shapes=[
            vmem(F32, *norm_gain.shape), vmem(F32, *bias_hidden.shape), vmem(F32, *gate_logit.shape),
            vmem(F32, *w_in.shape), vmem(F32, *w_out.shape),
            *[vmem(BF, w.shape[1] // 128, w.shape[0], 128) for w in (w_in, w_in, w_out, w_out)],
            vmem(F32, half, wide), vmem(F32, 2, half, wide), vmem(F32, 2, 2 * half, 128),
            vmem(F32, 2 * half, 128), vmem(F32, 2 * half, 128), vmem(F32, 2 * rows, 128), vmem(F32, 3, 8, 128),
            sem((7,)), sem((2,)), sem((2, 2)), sem((2, 2)),
        ],
        compiler_params=pltpu.CompilerParams(collective_id=0, has_side_effects=True, vmem_limit_bytes=40 << 20),
    )(*[pltpu.with_memory_space_constraint(a, pltpu.HBM) for a in (features, norm_gain, bias_hidden, gate_logit, w_in, w_out)])


def solution(mesh):
    placed = (P(("seqhi", "seqlo"), None), P(), P(), P(), P(), P())
    return jax.shard_map(body, mesh=mesh, in_specs=placed, out_specs=P(("seqhi", "seqlo"), None), check_vma=False)
```

```python
import math

import jax
import jax.numpy as jnp
from jax import lax
from jax.experimental import pallas as pl
from jax.experimental.pallas import tpu as pltpu
from jax.sharding import PartitionSpec as P

MESH = pl.DeviceIdType.MESH
BF, F32 = jnp.bfloat16, jnp.float32
NORM_EPS = 1e-05
GELU_A = (2 / math.pi) ** 0.5
GELU_B = GELU_A * 0.044715
Z, ZLO, X = 16, 8, 4
SHARED = 1


def ring_order(size):
    order = []
    for step in range(size):
        half = (step + 1) // 2
        order.append((size // 2 - half if step % 2 else size // 2 + half) % size)
    return order


def chips(hi, lo, turns_z, at_y=None):
    z_lo, x, z_hi, y = lax.div(hi, 2), lax.rem(lo, 4), lax.rem(lax.div(lo, 4), 2), lax.rem(lax.div(lo, 8), 2)
    block = lo - lax.rem(lo, 16)
    z = z_hi * ZLO + z_lo
    along_x = []
    for dx in (2, 1, 3, 0):
        to = lax.rem(x + dx, X)
        along_x.append((to, lax.rem(to, 2) * 8 + lax.div(to, 2) * 4))
    along_y = [1 - y, y] if at_y is None else at_y
    found = []
    for dz in turns_z:
        to = lax.rem(z + dz, Z)
        to_hi, to_lo = lax.div(to, ZLO), lax.rem(to, ZLO)
        place_z = lax.rem(to_lo, 2) * 64 + lax.rem(lax.div(to_lo, 2), 2) * 32 + lax.div(to_lo, 4) * 16 + to_hi * 2
        at_z = block + to_hi * 4
        for to_x, place_x in along_x:
            for to_y in along_y:
                found.append((to_lo, at_z + to_x + to_y * 8, place_z + place_x + to_y))
    return found


def gelu(value):
    inner = value * (GELU_A + GELU_B * (value * value))
    half = 0.5 * value
    return half + half * jnp.tanh(inner)


def halves(value):
    high = value.astype(BF)
    return high, (value - high.astype(F32)).astype(BF)


def product(value, weight_high, weight_low, beside=lambda columns: None):
    rows = value.shape[0]
    high, low = halves(value)
    stacked = jnp.concatenate([high, low], 0)
    columns = []
    for block in range(0, weight_high.shape[0], 2):
        tile_high = jnp.concatenate([weight_high[block], weight_high[block + 1]], -1)
        tile_low = jnp.concatenate([weight_low[block], weight_low[block + 1]], -1)
        both = jnp.dot(stacked, tile_high, preferred_element_type=F32)
        columns.append(both[:rows] + both[rows:] + jnp.dot(high, tile_low, preferred_element_type=F32))
        beside(columns)
    return jnp.concatenate(columns, -1)


def switch(pairs, params, done):
    gain, bias, gate, w_in, w_out = params
    wide = pairs[0][0].shape[-1]
    rows = pairs[0][0].shape[0]
    normed = []
    for lower, upper, layer in pairs:
        mean = (jnp.sum(lower, -1, keepdims=True) + jnp.sum(upper, -1, keepdims=True)) * (0.5 / wide)
        lower_c, upper_c = lower - mean, upper - mean
        spread = (jnp.sum(lower_c * lower_c, -1, keepdims=True) + jnp.sum(upper_c * upper_c, -1, keepdims=True)) * (0.5 / wide)
        scale = lax.rsqrt(spread + NORM_EPS)
        normed.append(jnp.concatenate([lower_c * scale, upper_c * scale], -1) * gain[pl.ds(layer, 1), :])
    inner = product(jnp.concatenate(normed, 0), *w_in)
    hidden = [gelu(inner[i * rows : i * rows + rows] + bias[pl.ds(layer, 1), :]) for i, (_, _, layer) in enumerate(pairs)]
    kept = [jax.nn.sigmoid(gate[pl.ds(layer, 1), :]) for _, _, layer in pairs]

    def finish(columns):
        side = len(columns) - 1
        for i, pair in enumerate(pairs):
            done(i, side, kept[i][:, side * wide : side * wide + wide] * pair[side] + columns[side][i * rows : i * rows + rows])

    product(jnp.concatenate(hidden, 0), *w_out, finish)


def pair_layers(instances, params, after=lambda side: None):
    pairs = []
    for points, layer in instances:
        rows = points.shape[0] // 4
        lower = jnp.concatenate([points[pl.ds(part, rows, stride=2), :] for part in range(2)], -1)
        upper = jnp.concatenate([points[pl.ds(2 * rows + part, rows, stride=2), :] for part in range(2)], -1)
        pairs.append((lower, upper, layer))

    def done(i, side, value):
        points = instances[i][0]
        for part in range(2):
            points[pl.ds(2 * side + part, rows, stride=4), :] = value[:, part * 128 : part * 128 + 128]
        if i == len(pairs) - 1:
            after(side)

    switch(pairs, params, done)


def split_weight(whole, high, low):
    rows = whole.shape[0]

    def step(index, carry):
        at = pl.ds(pl.multiple_of(index * 64, 64), 64)
        for block in range(high.shape[0]):
            high[block, at, :], low[block, at, :] = halves(whole[at, block * 128 : block * 128 + 128])
        return carry

    lax.fori_loop(0, rows // 64, step, 0)


def row_at(place):
    return pl.ds(pl.multiple_of(2 * place, 2), 2)


def took(ref, sem):
    pltpu.make_async_copy(ref, ref, sem).wait()


def kernel(
    x_hbm, gain_hbm, bias_hbm, gate_hbm, w_in_hbm, w_out_hbm, out,
    gain, bias, gate, w_in, w_out, in_high, in_low, out_high, out_low,
    away, paired, mixed, points_a, points_b, arrived, spare, loads, core_sem, in_sem, out_sem,
):
    hi, lo = lax.axis_index("seqhi"), lax.axis_index("seqlo")
    core = lax.rem(hi, 2)
    other = 1 - core
    peers = chips(hi, lo, ring_order(Z))
    my_place = peers[-1][2]
    layers = gain.shape[0]
    half = paired.shape[1]

    barrier = pltpu.get_barrier_semaphore()
    for z_lo, to_lo, _ in peers[:-1]:
        pl.semaphore_signal(barrier, inc=1, device_id=(z_lo * 2 + core, to_lo), device_id_type=MESH)
    partner = (hi + 1 - 2 * core, lo)
    pl.semaphore_signal(barrier, inc=1, device_id=partner, device_id_type=MESH)

    keep_at = pl.ds(pl.multiple_of(core * half, half), half)
    send_at = pl.ds(pl.multiple_of(other * half, half), half)
    fetched = [
        pltpu.make_async_copy(source, target, loads.at[index])
        for index, (source, target) in enumerate(
            [
                (w_in_hbm, w_in), (w_out_hbm, w_out), (gain_hbm, gain), (bias_hbm, bias), (gate_hbm, gate),
                (x_hbm.at[send_at, :], away), (x_hbm.at[keep_at, :], paired.at[core]),
            ]
        )
    ]
    for copy in fetched:
        copy.start()
    fetched[0].wait()
    split_weight(w_in, in_high, in_low)
    fetched[1].wait()
    split_weight(w_out, out_high, out_low)
    for copy in fetched[2:]:
        copy.wait()
    params = (gain, bias, gate, (in_high, in_low), (out_high, out_low))

    pl.semaphore_wait(barrier, len(peers))
    quarter = half // 2
    odd = lax.rem(lax.div(hi, 2), 2)
    parts_at = [pl.multiple_of(index * quarter, quarter) for index in (odd, 1 - odd)]
    swaps = [
        pltpu.make_async_remote_copy(
            src_ref=away.at[pl.ds(at, quarter), :], dst_ref=paired.at[core, pl.ds(at, quarter), :],
            send_sem=core_sem.at[0, index], recv_sem=core_sem.at[1, index],
            device_id=partner, device_id_type=MESH,
        )
        for index, at in enumerate(parts_at)
    ]
    for swap in swaps:
        swap.start()
    targets = (points_a, points_b)

    def gather(which, peer):
        z_lo, to_lo, place = peer
        pltpu.make_async_remote_copy(
            src_ref=mixed.at[core if which == 0 else other, row_at(place), :], dst_ref=targets[which].at[row_at(my_place), :],
            send_sem=in_sem.at[0, which], recv_sem=in_sem.at[1, which],
            device_id=(z_lo * 2 + core, to_lo), device_id_type=MESH,
        ).start()

    for index, at in enumerate(parts_at):
        swaps[index].wait()

        def mix(_, side, value):
            for part in range(2):
                mixed[side, pl.ds(2 * at + part, quarter, stride=2), :] = value[:, part * 128 : part * 128 + 128]

        switch([(paired[0, pl.ds(at, quarter), :], paired[1, pl.ds(at, quarter), :], 0)], params, mix)
        turns = [turn for turn in ring_order(Z) if turn % 2 == index]
        found = chips(hi, lo, turns)
        for peer in found[:-1] if index == 0 else found:
            gather(0, peer)
    for peer in peers[:-1]:
        gather(1, peer)
    for which, points in enumerate(targets):
        own = mixed.at[core if which == 0 else other, row_at(my_place), :]
        pltpu.make_async_copy(own, points.at[row_at(my_place), :], in_sem.at[1, which]).start()
        pltpu.make_async_copy(own, spare.at[which, pl.ds(0, 2), :], in_sem.at[0, which]).start()

    home = row_at(core * half + my_place)

    def send_home(which, points, peer):
        z_lo, to_lo, place = peer
        pltpu.make_async_remote_copy(
            src_ref=points.at[row_at(place), :], dst_ref=arrived.at[home, :],
            send_sem=out_sem.at[0, which], recv_sem=out_sem.at[1, which],
            device_id=(z_lo * 2 + (core if which == 0 else other), to_lo), device_id_type=MESH,
        ).start()

    took(points_a, in_sem.at[1, 0])

    def alone(points, first, end):
        def step(layer, carry):
            pair_layers([(points, layer)], params)
            return carry

        lax.fori_loop(first, end, step, 0)

    def together(layer, carry):
        pair_layers([(points_a, layer), (points_b, layer + SHARED + 1 - layers)], params)
        return carry

    alone(points_a, 1, layers - SHARED)
    took(points_b, in_sem.at[1, 1])
    lax.fori_loop(layers - SHARED, layers, together, 0)
    own = points_a.at[row_at(my_place), :]
    pltpu.make_async_copy(own, arrived.at[home, :], out_sem.at[1, 0]).start()
    pltpu.make_async_copy(own, spare.at[2, pl.ds(0, 2), :], out_sem.at[0, 0]).start()
    for peer in peers[:-1]:
        send_home(0, points_a, peer)
    alone(points_b, SHARED + 1, layers - 1)
    by_y = [chips(hi, lo, ring_order(Z), (side,)) for side in range(2)]

    def leave(side):
        for peer in by_y[side]:
            send_home(1, points_b, peer)

    pair_layers([(points_b, layers - 1)], params, leave)

    for which, points in enumerate((points_a, points_b)):
        took(points, in_sem.at[0, which])
        took(points, out_sem.at[0, which])
    took(arrived.at[pl.ds(0, 2 * half), :], out_sem.at[1, 0])
    took(arrived.at[pl.ds(0, 2 * half), :], out_sem.at[1, 1])
    for part in range(2):
        out[:, part * 128 : part * 128 + 128] = arrived[pl.ds(part, 2 * half, stride=2), :]


def body(features, norm_gain, bias_hidden, gate_logit, w_in, w_out):
    rows, wide = features.shape
    half = rows // 2
    anywhere = pl.BlockSpec(memory_space=pltpu.HBM)
    sem = pltpu.SemaphoreType.DMA
    vmem = lambda dtype, *shape: pltpu.VMEM(shape, dtype)
    return pl.pallas_call(
        kernel,
        out_shape=jax.ShapeDtypeStruct((rows, wide), F32),
        in_specs=[anywhere] * 6,
        out_specs=pl.BlockSpec(memory_space=pltpu.VMEM),
        scratch_shapes=[
            vmem(F32, *norm_gain.shape), vmem(F32, *bias_hidden.shape), vmem(F32, *gate_logit.shape),
            vmem(F32, *w_in.shape), vmem(F32, *w_out.shape),
            *[vmem(BF, w.shape[1] // 128, w.shape[0], 128) for w in (w_in, w_in, w_out, w_out)],
            vmem(F32, half, wide), vmem(F32, 2, half, wide), vmem(F32, 2, 2 * half, 128),
            vmem(F32, 2 * half, 128), vmem(F32, 2 * half, 128), vmem(F32, 2 * rows, 128), vmem(F32, 3, 8, 128),
            sem((7,)), sem((2, 2)), sem((2, 2)), sem((2, 2)),
        ],
        compiler_params=pltpu.CompilerParams(collective_id=0, has_side_effects=True, vmem_limit_bytes=40 << 20),
    )(*[pltpu.with_memory_space_constraint(a, pltpu.HBM) for a in (features, norm_gain, bias_hidden, gate_logit, w_in, w_out)])


def solution(mesh):
    placed = (P(("seqhi", "seqlo"), None), P(), P(), P(), P(), P())
    return jax.shard_map(body, mesh=mesh, in_specs=placed, out_specs=P(("seqhi", "seqlo"), None), check_vma=False)
```

```python
import math

import jax
import jax.numpy as jnp
from jax import lax
from jax.experimental import pallas as pl
from jax.experimental.pallas import tpu as pltpu
from jax.sharding import PartitionSpec as P

MESH = pl.DeviceIdType.MESH
BF, F32 = jnp.bfloat16, jnp.float32
NORM_EPS = 1e-05
GELU_A = (2 / math.pi) ** 0.5
GELU_B = GELU_A * 0.044715
Z, ZLO, X = 16, 8, 4
SHARED = 2


def ring_order(size):
    order = []
    for step in range(size):
        half = (step + 1) // 2
        order.append((size // 2 - half if step % 2 else size // 2 + half) % size)
    return order


def chips(hi, lo, turns_z, at_y=None):
    z_lo, x, z_hi, y = lax.div(hi, 2), lax.rem(lo, 4), lax.rem(lax.div(lo, 4), 2), lax.rem(lax.div(lo, 8), 2)
    block = lo - lax.rem(lo, 16)
    z = z_hi * ZLO + z_lo
    along_x = []
    for dx in (2, 1, 3, 0):
        to = lax.rem(x + dx, X)
        along_x.append((to, lax.rem(to, 2) * 8 + lax.div(to, 2) * 4))
    along_y = [1 - y, y] if at_y is None else at_y
    found = []
    for dz in turns_z:
        to = lax.rem(z + dz, Z)
        to_hi, to_lo = lax.div(to, ZLO), lax.rem(to, ZLO)
        place_z = lax.rem(to_lo, 2) * 64 + lax.rem(lax.div(to_lo, 2), 2) * 32 + lax.div(to_lo, 4) * 16 + to_hi * 2
        at_z = block + to_hi * 4
        for to_x, place_x in along_x:
            for to_y in along_y:
                found.append((to_lo, at_z + to_x + to_y * 8, place_z + place_x + to_y))
    return found


def gelu(value):
    inner = value * (GELU_A + GELU_B * (value * value))
    half = 0.5 * value
    return half + half * jnp.tanh(inner)


def halves(value):
    high = value.astype(BF)
    return high, (value - high.astype(F32)).astype(BF)


def product(value, weight_high, weight_low, beside=lambda columns: None):
    rows = value.shape[0]
    high, low = halves(value)
    stacked = jnp.concatenate([high, low], 0)
    columns = []
    for block in range(0, weight_high.shape[0], 2):
        tile_high = jnp.concatenate([weight_high[block], weight_high[block + 1]], -1)
        tile_low = jnp.concatenate([weight_low[block], weight_low[block + 1]], -1)
        both = jnp.dot(stacked, tile_high, preferred_element_type=F32)
        columns.append(both[:rows] + both[rows:] + jnp.dot(high, tile_low, preferred_element_type=F32))
        beside(columns)
    return jnp.concatenate(columns, -1)


def switch(pairs, params, done):
    gain, bias, gate, w_in, w_out = params
    wide = pairs[0][0].shape[-1]
    rows = pairs[0][0].shape[0]
    normed = []
    for lower, upper, layer in pairs:
        mean = (jnp.sum(lower, -1, keepdims=True) + jnp.sum(upper, -1, keepdims=True)) * (0.5 / wide)
        lower_c, upper_c = lower - mean, upper - mean
        spread = (jnp.sum(lower_c * lower_c, -1, keepdims=True) + jnp.sum(upper_c * upper_c, -1, keepdims=True)) * (0.5 / wide)
        scale = lax.rsqrt(spread + NORM_EPS)
        normed.append(jnp.concatenate([lower_c * scale, upper_c * scale], -1) * gain[pl.ds(layer, 1), :])
    inner = product(jnp.concatenate(normed, 0), *w_in)
    hidden = [gelu(inner[i * rows : i * rows + rows] + bias[pl.ds(layer, 1), :]) for i, (_, _, layer) in enumerate(pairs)]
    kept = [jax.nn.sigmoid(gate[pl.ds(layer, 1), :]) for _, _, layer in pairs]

    def finish(columns):
        side = len(columns) - 1
        for i, pair in enumerate(pairs):
            done(i, side, kept[i][:, side * wide : side * wide + wide] * pair[side] + columns[side][i * rows : i * rows + rows])

    product(jnp.concatenate(hidden, 0), *w_out, finish)


def pair_layers(instances, params, after=lambda side: None):
    pairs = []
    for points, layer in instances:
        rows = points.shape[0] // 4
        lower = jnp.concatenate([points[pl.ds(part, rows, stride=2), :] for part in range(2)], -1)
        upper = jnp.concatenate([points[pl.ds(2 * rows + part, rows, stride=2), :] for part in range(2)], -1)
        pairs.append((lower, upper, layer))

    def done(i, side, value):
        points = instances[i][0]
        for part in range(2):
            points[pl.ds(2 * side + part, rows, stride=4), :] = value[:, part * 128 : part * 128 + 128]
        if i == len(pairs) - 1:
            after(side)

    switch(pairs, params, done)


def split_weight(whole, high, low):
    rows = whole.shape[0]

    def step(index, carry):
        at = pl.ds(pl.multiple_of(index * 64, 64), 64)
        for block in range(high.shape[0]):
            high[block, at, :], low[block, at, :] = halves(whole[at, block * 128 : block * 128 + 128])
        return carry

    lax.fori_loop(0, rows // 64, step, 0)


def row_at(place):
    return pl.ds(pl.multiple_of(2 * place, 2), 2)


def took(ref, sem):
    pltpu.make_async_copy(ref, ref, sem).wait()


def kernel(
    x_hbm, gain_hbm, bias_hbm, gate_hbm, w_in_hbm, w_out_hbm, out,
    gain, bias, gate, w_in, w_out, in_high, in_low, out_high, out_low,
    away, paired, mixed, points_a, points_b, arrived, spare, loads, core_sem, in_sem, out_sem,
):
    hi, lo = lax.axis_index("seqhi"), lax.axis_index("seqlo")
    core = lax.rem(hi, 2)
    other = 1 - core
    peers = chips(hi, lo, ring_order(Z))
    my_place = peers[-1][2]
    layers = gain.shape[0]
    half = paired.shape[1]

    barrier = pltpu.get_barrier_semaphore()
    for z_lo, to_lo, _ in peers[:-1]:
        pl.semaphore_signal(barrier, inc=1, device_id=(z_lo * 2 + core, to_lo), device_id_type=MESH)
    partner = (hi + 1 - 2 * core, lo)
    pl.semaphore_signal(barrier, inc=1, device_id=partner, device_id_type=MESH)

    keep_at = pl.ds(pl.multiple_of(core * half, half), half)
    send_at = pl.ds(pl.multiple_of(other * half, half), half)
    fetched = [
        pltpu.make_async_copy(source, target, loads.at[index])
        for index, (source, target) in enumerate(
            [
                (w_in_hbm, w_in), (w_out_hbm, w_out), (gain_hbm, gain), (bias_hbm, bias), (gate_hbm, gate),
                (x_hbm.at[send_at, :], away), (x_hbm.at[keep_at, :], paired.at[core]),
            ]
        )
    ]
    for copy in fetched:
        copy.start()
    fetched[0].wait()
    split_weight(w_in, in_high, in_low)
    fetched[1].wait()
    split_weight(w_out, out_high, out_low)
    for copy in fetched[2:]:
        copy.wait()
    params = (gain, bias, gate, (in_high, in_low), (out_high, out_low))

    pl.semaphore_wait(barrier, len(peers))
    swap = pltpu.make_async_remote_copy(
        src_ref=away, dst_ref=paired.at[core], send_sem=core_sem.at[0], recv_sem=core_sem.at[1],
        device_id=partner, device_id_type=MESH,
    )
    swap.start()
    swap.wait()

    def mix(_, side, value):
        for part in range(2):
            mixed[side, pl.ds(part, half, stride=2), :] = value[:, part * 128 : part * 128 + 128]

    switch([(paired[0], paired[1], 0)], params, mix)

    for which, points in enumerate((points_a, points_b)):
        whose = core if which == 0 else other
        for z_lo, to_lo, place in peers[:-1]:
            pltpu.make_async_remote_copy(
                src_ref=mixed.at[whose, row_at(place), :], dst_ref=points.at[row_at(my_place), :],
                send_sem=in_sem.at[0, which], recv_sem=in_sem.at[1, which],
                device_id=(z_lo * 2 + core, to_lo), device_id_type=MESH,
            ).start()
        own = mixed.at[whose, row_at(my_place), :]
        pltpu.make_async_copy(own, points.at[row_at(my_place), :], in_sem.at[1, which]).start()
        pltpu.make_async_copy(own, spare.at[which, pl.ds(0, 2), :], in_sem.at[0, which]).start()

    home = row_at(core * half + my_place)

    def send_home(which, points, peer):
        z_lo, to_lo, place = peer
        pltpu.make_async_remote_copy(
            src_ref=points.at[row_at(place), :], dst_ref=arrived.at[home, :],
            send_sem=out_sem.at[0, which], recv_sem=out_sem.at[1, which],
            device_id=(z_lo * 2 + (core if which == 0 else other), to_lo), device_id_type=MESH,
        ).start()

    took(points_a, in_sem.at[1, 0])

    def alone(points, first, end):
        def step(layer, carry):
            pair_layers([(points, layer)], params)
            return carry

        lax.fori_loop(first, end, step, 0)

    def together(layer, carry):
        pair_layers([(points_a, layer), (points_b, layer + SHARED + 1 - layers)], params)
        return carry

    alone(points_a, 1, layers - SHARED)
    took(points_b, in_sem.at[1, 1])
    lax.fori_loop(layers - SHARED, layers, together, 0)
    own = points_a.at[row_at(my_place), :]
    pltpu.make_async_copy(own, arrived.at[home, :], out_sem.at[1, 0]).start()
    pltpu.make_async_copy(own, spare.at[2, pl.ds(0, 2), :], out_sem.at[0, 0]).start()
    far = [turn for turn in ring_order(Z) if turn not in (Z - 1, 1, 0)]
    for peer in chips(hi, lo, far):
        send_home(0, points_a, peer)
    alone(points_b, SHARED + 1, layers - 1)
    by_y = [chips(hi, lo, ring_order(Z), (side,)) for side in range(2)]

    def leave(side):
        for peer in by_y[side]:
            send_home(1, points_b, peer)

    pair_layers([(points_b, layers - 1)], params, leave)
    for peer in chips(hi, lo, (Z - 1, 1, 0))[:-1]:
        send_home(0, points_a, peer)

    for which, points in enumerate((points_a, points_b)):
        took(points, in_sem.at[0, which])
        took(points, out_sem.at[0, which])
    took(arrived.at[pl.ds(0, 2 * half), :], out_sem.at[1, 0])
    took(arrived.at[pl.ds(0, 2 * half), :], out_sem.at[1, 1])
    for part in range(2):
        out[:, part * 128 : part * 128 + 128] = arrived[pl.ds(part, 2 * half, stride=2), :]


def body(features, norm_gain, bias_hidden, gate_logit, w_in, w_out):
    rows, wide = features.shape
    half = rows // 2
    anywhere = pl.BlockSpec(memory_space=pltpu.HBM)
    sem = pltpu.SemaphoreType.DMA
    vmem = lambda dtype, *shape: pltpu.VMEM(shape, dtype)
    return pl.pallas_call(
        kernel,
        out_shape=jax.ShapeDtypeStruct((rows, wide), F32),
        in_specs=[anywhere] * 6,
        out_specs=pl.BlockSpec(memory_space=pltpu.VMEM),
        scratch_shapes=[
            vmem(F32, *norm_gain.shape), vmem(F32, *bias_hidden.shape), vmem(F32, *gate_logit.shape),
            vmem(F32, *w_in.shape), vmem(F32, *w_out.shape),
            *[vmem(BF, w.shape[1] // 128, w.shape[0], 128) for w in (w_in, w_in, w_out, w_out)],
            vmem(F32, half, wide), vmem(F32, 2, half, wide), vmem(F32, 2, 2 * half, 128),
            vmem(F32, 2 * half, 128), vmem(F32, 2 * half, 128), vmem(F32, 2 * rows, 128), vmem(F32, 3, 8, 128),
            sem((7,)), sem((2,)), sem((2, 2)), sem((2, 2)),
        ],
        compiler_params=pltpu.CompilerParams(collective_id=0, has_side_effects=True, vmem_limit_bytes=40 << 20),
    )(*[pltpu.with_memory_space_constraint(a, pltpu.HBM) for a in (features, norm_gain, bias_hidden, gate_logit, w_in, w_out)])


def solution(mesh):
    placed = (P(("seqhi", "seqlo"), None), P(), P(), P(), P(), P())
    return jax.shard_map(body, mesh=mesh, in_specs=placed, out_specs=P(("seqhi", "seqlo"), None), check_vma=False)
```
